128 devices in a mesh: row: 8 (over x, core), col: 16 (over y, z).
Axes of the slice: x: 4, y: 4, z: 4, core: 2. Of those that a mesh axis runs over, the one named last changes fastest.
Arguments:
- adjacency: bfloat16 [8192, 65536], P('row', 'col'), may hold values from -0.03125 to 0.03125
- tile_mask: int32 [32, 256], P('row', 'col'), may hold values from 0 to 1, as said below
- operand: bfloat16 [65536, 2048], P('col'), may hold values from -6 to 6
- current: bfloat16 [8192, 2048], P('row', 'col'), may hold values from 0 to 1
Outputs:
- reached: bfloat16 [8192, 2048], P('row', 'col')
- progress: float32 [32], P('row')
The draws below stay inside these ranges and needn't reach their ends.
Inputs may be any that keep to these rules, and one draw needn't show every extreme that they name: Split tile_mask into blocks of 4 tile rows by 16 tile columns, aligned to multiples of these. Every block holds at least one nonzero tile, and a block together with the block in the same tile columns whose tile rows start 16 tile rows farther down (upper half of the slab paired with lower half, in order) holds exactly 64 nonzero tiles.
All inputs are finite; a program needn't handle non-finite values.
Results may differ from the reference program's by a relative error of at most 0.0045.
Values may be sent and summed in bfloat16 or wider, within the bound.
No kernel may reach another device: no remote copies, remote signals or barrier semaphores. Data moves between devices by JAX's collectives and lax.ppermute only.
A program may use at most 128 MiB of HBM per device.

```python
import jax
import jax.numpy as jnp

TILE = 256
N = 65536
TR_DEV = 4
TR = 32
W = 2048
TILES_DEV = 16


def draw_tile_mask(key, part):
    n_rows = TR // TR_DEV
    n_cols = N // TILE // TILES_DEV
    capacity = TR_DEV * TILES_DEV
    half_rows = n_rows // 2
    lowest = max(1, capacity // 11)
    upper_counts = jax.random.randint(jax.random.fold_in(key, 11), (half_rows, n_cols), lowest, capacity - lowest + 1)
    counts = jnp.concatenate([upper_counts, capacity - upper_counts], axis=0)
    scores = jax.random.randint(jax.random.fold_in(key, 23), (n_rows, n_cols, capacity), 0, 1048576) * capacity
    scores = scores + jnp.arange(capacity, dtype=jnp.int32)[None, None, :]
    ranks = jnp.argsort(jnp.argsort(scores, axis=-1), axis=-1).astype(jnp.int32)
    nonzero = (ranks < counts[:, :, None]).astype(jnp.int32)
    nonzero = nonzero.reshape(n_rows, n_cols, TR_DEV, TILES_DEV).transpose(0, 2, 1, 3)
    return nonzero.reshape(TR, N // TILE)


def steps_of(rng, dims, shards, least, top_value):
    level, own = 1.0, jax.random.fold_in(rng, 6)
    for dim, parts in shards:
        steps = jnp.exp(jax.random.uniform(jax.random.fold_in(own, dim), (parts,), jnp.float32, least / len(shards), top_value / len(shards)))
        level = level * jnp.repeat(steps, dims[dim] // parts).reshape([-1 if axis == dim else 1 for axis in range(len(dims))])
    return level


def scatter_about(rng, dims, scale, limit, cuts=(), held_as=jnp.bfloat16):
    result = scale * jax.random.normal(rng, dims, jnp.float32)
    if cuts:
        result = result * steps_of(rng, dims, cuts, -0.22, 0.18)
    return jnp.clip(result, -limit, limit).astype(held_as)


def setup_inputs(seed: int = 0) -> dict:
    key_list = jax.random.split(jax.random.key(seed), 5)
    return {
        "adjacency": scatter_about(key_list[0], (TR * TILE, N), (N // 2) ** -0.5, 0.03125, ((0, 8), (1, 16))),
        "tile_mask": draw_tile_mask(jax.random.fold_in(key_list[4], 71), 0),
        "operand": scatter_about(key_list[2], (N, W), 1.0, 6.0, ((0, 16),)),
        "current": jnp.clip(1.0 * jax.random.uniform(key_list[3], (TR * TILE, W), jnp.float32) ** steps_of(key_list[3], (TR * TILE, W), ((0, 8), (1, 16)), -0.2, 0.2), 0.0, 1.0).astype(jnp.bfloat16),
    }


def reference(adjacency, tile_mask, operand, current):
    row_count, col_count = adjacency.shape
    tiles_rows = row_count // TILE
    tiles_cols = col_count // TILE
    keep_tile = tile_mask.astype(jnp.bfloat16)[:, None, :, None]
    masked = (adjacency.reshape(tiles_rows, TILE, tiles_cols, TILE) * keep_tile).reshape(row_count, col_count)
    logits = jnp.dot(masked, operand, preferred_element_type=jnp.float32)
    prior_value = current.astype(jnp.float32)
    lifted = (1.0 - prior_value) * jax.nn.sigmoid(logits)
    reached = (prior_value + lifted).astype(jnp.bfloat16)
    window = operand.shape[1]
    row_gain = jnp.sum(lifted.reshape(tiles_rows, TILE * window), axis=1) / (TILE * window)
    progress = jnp.cumsum(row_gain)
    return reached, progress
```

```python
import jax
import jax.numpy as jnp
from jax import lax
from jax.experimental import pallas as pl
from jax.experimental.pallas import tpu as pltpu
from jax.sharding import Mesh
from jax.sharding import PartitionSpec as P

TILE = 256
COL = ("col_0", "col_1")
ALL = ("row", "col_0", "col_1")
ROWS, DEPTH, COLS, LANES = 1024, 4096, 2048, 128
HALF = ROWS // 2
GROUP = 4 * LANES
KB = 512
F32, BF16 = jnp.float32, jnp.bfloat16
VMEM_LIMIT = 24 * 1024 * 1024


def column_block(pos, first, second):
    core, y, z = pos[0], pos[1], pos[2]
    by_y = core == 0
    dy = jnp.where(by_y, first, second)
    dz = jnp.where(by_y, second, first)
    return ((y + dy) & 3) * 4 + ((z + dz) & 3)


def moved(x, first, second):
    pairs = []
    for dev in range(128):
        row, y, z = dev // 16, dev // 4 % 4, dev % 4
        dy, dz = (first, second) if row % 2 == 0 else (second, first)
        pairs.append((dev, row * 16 + (y + dy) % 4 * 4 + (z + dz) % 4))
    return lax.ppermute(x, ALL, pairs)


def far_kernel(pos, mask, a, b0, b1, b2, b3, masked, out_a, out_b, acc):
    k = pl.program_id(0)
    per = KB // TILE
    rows = []
    for i in range(ROWS // TILE):
        tiles = []
        for j in range(per):
            keep = mask[i, k * per + j].astype(F32)
            tile = a[i * TILE:(i + 1) * TILE, j * TILE:(j + 1) * TILE]
            tiles.append(tile * jnp.full((TILE, TILE), keep, F32).astype(BF16))
        rows.append(jnp.concatenate(tiles, axis=1))
    kept = jnp.concatenate(rows, axis=0)
    masked[:, pl.ds(pl.multiple_of(k * KB, KB), KB)] = kept
    b = jnp.concatenate([b0[...], b1[...], b2[...], b3[...]], axis=1)
    part = jnp.dot(kept, b, preferred_element_type=F32)

    @pl.when(k == 0)
    def _():
        acc[...] = part

    @pl.when(jnp.logical_and(k > 0, k < DEPTH // KB - 1))
    def _():
        acc[...] += part

    @pl.when(k == DEPTH // KB - 1)
    def _():
        out_a[...] = (acc[:HALF] + part[:HALF]).astype(BF16)
        out_b[...] = (acc[HALF:] + part[HALF:]).astype(BF16)


def far_block(pos, mask, adjacency, operand):
    def b_spec(j):
        return pl.BlockSpec((KB, LANES), lambda k, pos: (k, column_block(pos, 2, j)))

    whole = pl.BlockSpec(memory_space=pltpu.VMEM)
    return pl.pallas_call(
        far_kernel,
        grid_spec=pltpu.PrefetchScalarGridSpec(
            num_scalar_prefetch=1,
            grid=(DEPTH // KB,),
            in_specs=[pl.BlockSpec(memory_space=pltpu.SMEM), pl.BlockSpec((ROWS, KB), lambda k, pos: (0, k))]
            + [b_spec(j) for j in range(4)],
            out_specs=[whole, whole, whole],
            scratch_shapes=[pltpu.VMEM((ROWS, GROUP), F32)],
        ),
        out_shape=[pltpu.VMEM((ROWS, DEPTH), BF16), pltpu.VMEM((HALF, GROUP), BF16), pltpu.VMEM((HALF, GROUP), BF16)],
        compiler_params=pltpu.CompilerParams(vmem_limit_bytes=VMEM_LIMIT),
        cost_estimate=pl.CostEstimate(flops=2 * ROWS * DEPTH * GROUP, transcendentals=0, bytes_accessed=12 << 20),
        name="far_block",
    )(pos, mask, adjacency, operand, operand, operand, operand)


def near_kernel(starts, merge, pos, masked, b0, b1, *rest):
    outs = rest[-2:]
    s = pl.program_id(0)
    b = jnp.concatenate([b0[...], b1[...]], axis=1)
    for part in (0, 1):
        for side in (0, 1):
            @pl.when(s == 2 * part + side)
            def _():
                lanes = slice(side * 2 * LANES, (side + 1) * 2 * LANES)
                block = jnp.dot(masked[starts[part]:starts[part] + HALF], b, preferred_element_type=F32)
                if merge:
                    block = block + rest[part][:, lanes].astype(F32)
                outs[part][:, lanes] = block.astype(BF16)


def near_blocks(pos, masked, operand, starts, arrived=()):
    def b_spec(j):
        return pl.BlockSpec(
            (DEPTH, LANES), lambda s, pos: (0, column_block(pos, jnp.where(s < 2, 1, 3), 2 * (s & 1) + j))
        )

    whole = pl.BlockSpec(memory_space=pltpu.VMEM)
    in_vmem = [pltpu.with_memory_space_constraint(x, pltpu.VMEM) for x in (masked, *arrived)]
    return pl.pallas_call(
        lambda *refs: near_kernel(starts, bool(arrived), *refs),
        grid_spec=pltpu.PrefetchScalarGridSpec(
            num_scalar_prefetch=1,
            grid=(4,),
            in_specs=[whole, b_spec(0), b_spec(1)] + [whole] * len(arrived),
            out_specs=[whole, whole],
        ),
        out_shape=[pltpu.VMEM((HALF, GROUP), BF16)] * 2,
        compiler_params=pltpu.CompilerParams(vmem_limit_bytes=VMEM_LIMIT),
        cost_estimate=pl.CostEstimate(flops=2 * ROWS * DEPTH * GROUP, transcendentals=0, bytes_accessed=8 << 20),
        name="near_merged" if arrived else "near_direct",
    )(pos, in_vmem[0], operand, operand, *in_vmem[1:])


def own_kernel(pos, masked, b0, b1, out):
    s = pl.program_id(0)
    b = jnp.concatenate([b0[...], b1[...]], axis=1)
    for side in (0, 1):
        @pl.when(s == side)
        def _():
            lanes = slice(side * 2 * LANES, (side + 1) * 2 * LANES)
            out[:, lanes] = jnp.dot(masked[...], b, preferred_element_type=F32)


def own_block(pos, masked, operand):
    def b_spec(j):
        return pl.BlockSpec((DEPTH, LANES), lambda s, pos: (0, column_block(pos, 0, 2 * s + j)))

    whole = pl.BlockSpec(memory_space=pltpu.VMEM)
    return pl.pallas_call(
        own_kernel,
        grid_spec=pltpu.PrefetchScalarGridSpec(
            num_scalar_prefetch=1, grid=(2,), in_specs=[whole, b_spec(0), b_spec(1)], out_specs=whole
        ),
        out_shape=pltpu.VMEM((ROWS, GROUP), F32),
        compiler_params=pltpu.CompilerParams(vmem_limit_bytes=VMEM_LIMIT),
        cost_estimate=pl.CostEstimate(flops=2 * ROWS * DEPTH * GROUP, transcendentals=0, bytes_accessed=4 << 20),
        name="own_block",
    )(pos, pltpu.with_memory_space_constraint(masked, pltpu.VMEM), operand, operand)


def second_kernel(own, next_a, back_a, back_b, next_b, mine, one, two, three):
    for part, (x, y) in enumerate(((next_a, back_a), (back_b, next_b))):
        rows = slice(part * HALF, (part + 1) * HALF)
        for j, out in enumerate((mine, one, two, three)):
            lanes = slice(j * LANES, (j + 1) * LANES)
            total = own[rows, lanes] + x[:, lanes].astype(F32) + y[:, lanes].astype(F32)
            out[rows, :] = total.astype(out.dtype)


def second_blocks(own, *arrived):
    whole = pl.BlockSpec(memory_space=pltpu.VMEM)
    return pl.pallas_call(
        second_kernel,
        in_specs=[whole] * 5,
        out_specs=[whole] * 4,
        out_shape=[pltpu.VMEM((ROWS, LANES), F32)] + [pltpu.VMEM((ROWS, LANES), BF16)] * 3,
        compiler_params=pltpu.CompilerParams(vmem_limit_bytes=VMEM_LIMIT),
        name="second_blocks",
    )(*(pltpu.with_memory_space_constraint(x, pltpu.VMEM) for x in (own, *arrived)))


def lift_kernel(mine, one, two, three, current, reached, gains):
    lane = lax.broadcasted_iota(jnp.int32, (1, LANES), 1)
    row = jnp.zeros((1, LANES), F32)
    for i in range(ROWS // TILE):
        rows = slice(i * TILE, (i + 1) * TILE)
        logits = mine[rows] + one[rows].astype(F32) + two[rows].astype(F32) + three[rows].astype(F32)
        prior = current[rows].astype(F32)
        lifted = (1.0 - prior) * jax.nn.sigmoid(logits)
        reached[rows, :] = (prior + lifted).astype(BF16)
        total = jnp.sum(jnp.sum(lifted, axis=0, keepdims=True), axis=1, keepdims=True)
        row = row + jnp.where(lane == i, total, 0.0)
    gains[...] = jnp.broadcast_to(row / (TILE * COLS), gains.shape)


def lift(mine, one, two, three, current):
    whole = pl.BlockSpec(memory_space=pltpu.VMEM)
    return pl.pallas_call(
        lift_kernel,
        in_specs=[whole] * 5,
        out_specs=[whole] * 2,
        out_shape=[jax.ShapeDtypeStruct((ROWS, LANES), BF16), jax.ShapeDtypeStruct((128, LANES), F32)],
        compiler_params=pltpu.CompilerParams(vmem_limit_bytes=VMEM_LIMIT),
        name="lift",
    )(mine, one, two, three, current)


def local(adjacency, tile_mask, operand, current):
    row = lax.axis_index("row")
    pos = jnp.stack([row & 1, lax.axis_index("col_0"), lax.axis_index("col_1")]).astype(jnp.int32)
    masked, far_a, far_b = far_block(pos, tile_mask, adjacency, operand)
    in_b = moved(far_b, 1, 0)
    in_a = moved(far_a, -1, 0)
    next_a, back_b = near_blocks(pos, masked, operand, (0, HALF))
    next_a = moved(next_a, 1, 0)
    back_b = moved(back_b, -1, 0)
    own = own_block(pos, masked, operand)
    next_b, back_a = near_blocks(pos, masked, operand, (HALF, 0), (in_b, in_a))
    next_b = moved(next_b, 1, 0)
    back_a = moved(back_a, -1, 0)
    mine, one, two, three = second_blocks(own, next_a, back_a, back_b, next_b)
    two = moved(two, 0, 2)
    one = moved(one, 0, 1)
    three = moved(three, 0, -1)
    reached, gains = lift(mine, one, two, three, current)
    gains = lax.all_to_all(gains, ALL, 0, 0, tiled=True)[:, :4]
    sender = lax.broadcasted_iota(jnp.int32, (128, 4, 4), 0) // 16
    earlier = lax.broadcasted_iota(jnp.int32, (128, 4, 4), 1) <= lax.broadcasted_iota(jnp.int32, (128, 4, 4), 2)
    counted = (sender < row) | ((sender == row) & earlier)
    progress = jnp.sum(jnp.where(counted, gains[:, :, None], 0.0), axis=(0, 1))
    return (reached, progress)


def solution(mesh):
    torus = Mesh(mesh.devices.reshape(mesh.shape["row"], 4, 4), ALL)
    in_specs = (P("row", COL), P("row", COL), P(COL, None), P("row", COL))
    out_specs = (P("row", COL), P("row"))
    return jax.shard_map(local, mesh=torus, in_specs=in_specs, out_specs=out_specs, check_vma=False)
```

```python
import jax
import jax.numpy as jnp
from jax import lax
from jax.experimental import pallas as pl
from jax.experimental.pallas import tpu as pltpu
from jax.sharding import Mesh
from jax.sharding import PartitionSpec as P

TILE = 256
COL = ("col_0", "col_1")
ALL = ("row", "col_0", "col_1")
ROWS, DEPTH, COLS, LANES = 1024, 4096, 2048, 128
GROUP = 4 * LANES
SIDE = 2 * LANES
STEPS = ((0, 512), (512, 512), (1024, 1024), (2048, 1024), (3072, 1024))
F32, BF16 = jnp.float32, jnp.bfloat16
VMEM_LIMIT = 16 * 1024 * 1024


def position():
    return lax.axis_index("row") & 1, lax.axis_index("col_0"), lax.axis_index("col_1")


def column_block(pos, first, second):
    core, y, z = pos
    dy = first + core * (second - first)
    dz = second + core * (first - second)
    return ((y + dy) & 3) * 4 + ((z + dz) & 3)


def moved(x, first, second):
    pairs = []
    for dev in range(128):
        row, y, z = dev // 16, dev // 4 % 4, dev % 4
        dy, dz = (first, second) if row % 2 == 0 else (second, first)
        pairs.append((dev, row * 16 + (y + dy) % 4 * 4 + (z + dz) % 4))
    return lax.ppermute(x, ALL, pairs)


def columns_in(operand, pos, blocks, depth, bbuf, sems):
    return [
        pltpu.make_async_copy(
            operand.at[pl.ds(*depth), pl.ds(pl.multiple_of(column_block(pos, *block) * LANES, LANES), LANES)],
            bbuf.at[pl.ds(*depth), pl.ds(j * LANES, LANES)],
            sems.at[j],
        )
        for j, block in enumerate(blocks)
    ]


FAR = ((2, 0), (2, 1), (2, 2), (2, 3))
DIRECT = ((1, 0), (1, 1), (3, 2), (3, 3))
MERGED = ((3, 0), (3, 1), (1, 2), (1, 3))
OWN = ((0, 0), (0, 1), (0, 2), (0, 3))


def far_kernel(mask_hbm, adjacency, operand, masked, out_a, out_b, ahead_0, ahead_1, bbuf, acc, mask, mask_sem, a_sems, b_sems, ahead_sems):
    mask_copy = pltpu.make_async_copy(mask_hbm, mask, mask_sem)
    mask_copy.start()
    pos = position()
    a_copies, b_copies = [], []
    for k, (start, size) in enumerate(STEPS):
        depth = pl.ds(start, size)
        a_copies.append(pltpu.make_async_copy(adjacency.at[:, depth], masked.at[:, depth], a_sems.at[k]))
        a_copies[k].start()
        b_copies.append(columns_in(operand, pos, FAR, (start, size), bbuf, b_sems.at[k]))
        for copy in b_copies[k]:
            copy.start()
    ahead_copies = columns_in(operand, pos, DIRECT, (0, DEPTH), ahead_0, ahead_sems.at[0])
    ahead_copies += columns_in(operand, pos, MERGED, (0, DEPTH), ahead_1, ahead_sems.at[1])
    mask_copy.wait()
    for k, (start, size) in enumerate(STEPS):
        a_copies[k].wait()
        for i in range(ROWS // TILE):
            for j in range(start // TILE, (start + size) // TILE):
                @pl.when(mask[i, j] == 0)
                def _():
                    masked[i * TILE:(i + 1) * TILE, j * TILE:(j + 1) * TILE] = jnp.zeros((TILE, TILE), BF16)
        for copy in b_copies[k]:
            copy.wait()
        if k == 2:
            for copy in ahead_copies:
                copy.start()
        depth = slice(start, start + size)
        for i in range(ROWS // TILE):
            rows = slice(i * TILE, (i + 1) * TILE)
            part = jnp.dot(masked[rows, depth], bbuf[depth, :], preferred_element_type=F32)
            if k == 0:
                acc[rows, :] = part
            elif k < len(STEPS) - 1:
                acc[rows, :] += part
            else:
                out_a[rows, :] = (acc[rows, :SIDE] + part[:, :SIDE]).astype(BF16)
                out_b[rows, :] = (acc[rows, SIDE:] + part[:, SIDE:]).astype(BF16)
    for copy in ahead_copies:
        copy.wait()


WHOLE = pl.BlockSpec(memory_space=pltpu.VMEM)
IN_HBM = pl.BlockSpec(memory_space=pltpu.HBM)
MM_FLOPS = 2 * ROWS * DEPTH * GROUP
COLUMNS = pltpu.VMEM((DEPTH, GROUP), BF16)


def pinned(space, *arrays):
    return [pltpu.with_memory_space_constraint(x, space) for x in arrays]


def far_block(tile_mask, adjacency, operand):
    return pl.pallas_call(
        far_kernel,
        in_specs=[IN_HBM] * 3,
        out_specs=[WHOLE] * 5,
        scratch_shapes=[
            COLUMNS,
            pltpu.VMEM((ROWS, GROUP), F32),
            pltpu.SMEM((ROWS // TILE, DEPTH // TILE), jnp.int32),
            pltpu.SemaphoreType.DMA,
            pltpu.SemaphoreType.DMA((len(STEPS),)),
            pltpu.SemaphoreType.DMA((len(STEPS), 4)),
            pltpu.SemaphoreType.DMA((2, 4)),
        ],
        out_shape=[pltpu.VMEM((ROWS, DEPTH), BF16)] + [pltpu.VMEM((ROWS, SIDE), BF16)] * 2 + [COLUMNS] * 2,
        compiler_params=pltpu.CompilerParams(vmem_limit_bytes=VMEM_LIMIT),
        cost_estimate=pl.CostEstimate(flops=MM_FLOPS, transcendentals=0, bytes_accessed=20 << 20),
        name="far_block",
    )(*pinned(pltpu.HBM, tile_mask, adjacency, operand))


def near_kernel(merge, masked, columns, *rest):
    arrived, outs = rest[:-2], rest[-2:]
    for i in range(ROWS // TILE):
        rows = slice(i * TILE, (i + 1) * TILE)
        both = jnp.dot(masked[rows], columns[...], preferred_element_type=F32)
        for part, out in enumerate(outs):
            block = both[:, part * SIDE:(part + 1) * SIDE]
            if merge:
                block = block + arrived[part][rows].astype(F32)
            out[rows, :] = block.astype(BF16)


def near_blocks(masked, columns, arrived=()):
    return pl.pallas_call(
        lambda *refs: near_kernel(bool(arrived), *refs),
        in_specs=[WHOLE] * (2 + len(arrived)),
        out_specs=[WHOLE] * 2,
        out_shape=[pltpu.VMEM((ROWS, SIDE), BF16)] * 2,
        compiler_params=pltpu.CompilerParams(vmem_limit_bytes=VMEM_LIMIT),
        cost_estimate=pl.CostEstimate(flops=MM_FLOPS, transcendentals=0, bytes_accessed=0),
        name="near_merged" if arrived else "near_direct",
    )(*pinned(pltpu.VMEM, masked, columns, *arrived))


def own_kernel(masked, operand, out, bbuf, sems):
    pos = position()
    copies = []
    for k, step in enumerate(STEPS):
        copies.append(columns_in(operand, pos, OWN, step, bbuf, sems.at[k]))
        for copy in copies[k]:
            copy.start()
    for k, (start, size) in enumerate(STEPS):
        for copy in copies[k]:
            copy.wait()
        depth = slice(start, start + size)
        block = jnp.dot(masked[:, depth], bbuf[depth, :], preferred_element_type=F32)
        if k == 0:
            out[...] = block
        else:
            out[...] += block


def own_block(masked, operand):
    return pl.pallas_call(
        own_kernel,
        in_specs=[WHOLE, IN_HBM],
        out_specs=WHOLE,
        scratch_shapes=[pltpu.VMEM((DEPTH, GROUP), BF16), pltpu.SemaphoreType.DMA((len(STEPS), 4))],
        out_shape=pltpu.VMEM((ROWS, GROUP), F32),
        compiler_params=pltpu.CompilerParams(vmem_limit_bytes=VMEM_LIMIT),
        cost_estimate=pl.CostEstimate(flops=MM_FLOPS, transcendentals=0, bytes_accessed=4 << 20),
        name="own_block",
    )(*pinned(pltpu.VMEM, masked), *pinned(pltpu.HBM, operand))


def second_kernel(own, next_a, back_a, back_b, next_b, mine, one, two, three):
    for j, out in enumerate((mine, one, two, three)):
        x, y = (next_a, back_a) if j < 2 else (back_b, next_b)
        side = slice(j % 2 * LANES, (j % 2 + 1) * LANES)
        total = own[:, j * LANES:(j + 1) * LANES] + x[:, side].astype(F32) + y[:, side].astype(F32)
        out[...] = total.astype(out.dtype)


def second_blocks(own, *arrived):
    return pl.pallas_call(
        second_kernel,
        in_specs=[WHOLE] * 5,
        out_specs=[WHOLE] * 4,
        out_shape=[pltpu.VMEM((ROWS, LANES), F32)] + [pltpu.VMEM((ROWS, LANES), BF16)] * 3,
        compiler_params=pltpu.CompilerParams(vmem_limit_bytes=VMEM_LIMIT),
        name="second_blocks",
    )(*pinned(pltpu.VMEM, own, *arrived))


def lift_kernel(mine, one, two, three, current, reached, gains):
    lane = lax.broadcasted_iota(jnp.int32, (1, LANES), 1)
    row = jnp.zeros((1, LANES), F32)
    for i in range(ROWS // TILE):
        rows = slice(i * TILE, (i + 1) * TILE)
        logits = mine[rows] + one[rows].astype(F32) + two[rows].astype(F32) + three[rows].astype(F32)
        prior = current[rows].astype(F32)
        lifted = (1.0 - prior) * jax.nn.sigmoid(logits)
        reached[rows, :] = (prior + lifted).astype(BF16)
        total = jnp.sum(jnp.sum(lifted, axis=0, keepdims=True), axis=1, keepdims=True)
        row = row + jnp.where(lane == i, total, 0.0)
    gains[...] = jnp.broadcast_to(row / (TILE * COLS), gains.shape)


def lift(mine, one, two, three, current):
    return pl.pallas_call(
        lift_kernel,
        in_specs=[WHOLE] * 5,
        out_specs=[WHOLE] * 2,
        out_shape=[jax.ShapeDtypeStruct((ROWS, LANES), BF16), jax.ShapeDtypeStruct((128, LANES), F32)],
        compiler_params=pltpu.CompilerParams(vmem_limit_bytes=VMEM_LIMIT),
        name="lift",
    )(mine, one, two, three, current)


def local(adjacency, tile_mask, operand, current):
    row = lax.axis_index("row")
    masked, far_a, far_b, columns, more_columns = far_block(tile_mask, adjacency, operand)
    in_b = moved(far_b, 1, 0)
    in_a = moved(far_a, -1, 0)
    next_a, back_b = near_blocks(masked, columns)
    next_a = moved(next_a, 1, 0)
    back_b = moved(back_b, -1, 0)
    back_a, next_b = near_blocks(masked, more_columns, (in_a, in_b))
    next_b = moved(next_b, 1, 0)
    back_a = moved(back_a, -1, 0)
    own = own_block(masked, operand)
    mine, one, two, three = second_blocks(own, next_a, back_a, back_b, next_b)
    two = moved(two, 0, 2)
    one = moved(one, 0, 1)
    three = moved(three, 0, -1)
    reached, gains = lift(mine, two, one, three, current)
    gains = lax.all_to_all(gains, ALL, 0, 0, tiled=True)[:, :4]
    sender = lax.broadcasted_iota(jnp.int32, (128, 4, 4), 0) // 16
    earlier = lax.broadcasted_iota(jnp.int32, (128, 4, 4), 1) <= lax.broadcasted_iota(jnp.int32, (128, 4, 4), 2)
    counted = (sender < row) | ((sender == row) & earlier)
    progress = jnp.sum(jnp.where(counted, gains[:, :, None], 0.0), axis=(0, 1))
    return (reached, progress)


def solution(mesh):
    torus = Mesh(mesh.devices.reshape(mesh.shape["row"], 4, 4), ALL)
    in_specs = (P("row", COL), P("row", COL), P(COL, None), P("row", COL))
    out_specs = (P("row", COL), P("row"))
    return jax.shard_map(local, mesh=torus, in_specs=in_specs, out_specs=out_specs, check_vma=False)
```

```python
import jax
import jax.numpy as jnp
from jax import lax
from jax.experimental import pallas as pl
from jax.experimental.pallas import tpu as pltpu
from jax.sharding import Mesh
from jax.sharding import PartitionSpec as P

TILE = 256
COL = ("col_0", "col_1")
ALL = ("row", "col_0", "col_1")
ROWS, DEPTH, COLS, LANES = 1024, 4096, 2048, 128
GROUP = 4 * LANES
SIDE = 2 * LANES
STEPS = ((0, 512), (512, 512), (1024, 1024), (2048, 1024), (3072, 1024))
F32, BF16 = jnp.float32, jnp.bfloat16
VMEM_LIMIT = 16 * 1024 * 1024


def position():
    return lax.axis_index("row") & 1, lax.axis_index("col_0"), lax.axis_index("col_1")


def column_block(pos, first, second):
    core, y, z = pos
    dy = first + core * (second - first)
    dz = second + core * (first - second)
    return ((y + dy) & 3) * 4 + ((z + dz) & 3)


def moved(x, first, second):
    pairs = []
    for dev in range(128):
        row, y, z = dev // 16, dev // 4 % 4, dev % 4
        dy, dz = (first, second) if row % 2 == 0 else (second, first)
        pairs.append((dev, row * 16 + (y + dy) % 4 * 4 + (z + dz) % 4))
    return lax.ppermute(x, ALL, pairs)


def columns_in(operand, pos, blocks, depth, bbuf, sems):
    return [
        pltpu.make_async_copy(
            operand.at[pl.ds(*depth), pl.ds(pl.multiple_of(column_block(pos, *block) * LANES, LANES), LANES)],
            bbuf.at[pl.ds(*depth), pl.ds(j * LANES, LANES)],
            sems.at[j],
        )
        for j, block in enumerate(blocks)
    ]


FAR = ((2, 0), (2, 2), (2, 1), (2, 3))
DIRECT = ((1, 0), (1, 2), (3, 1), (3, 3))
MERGED = ((3, 0), (3, 2), (1, 1), (1, 3))
OWN = ((0, 0), (0, 2), (0, 1), (0, 3))


def far_kernel(mask_hbm, adjacency, operand, masked, out_a, out_b, ahead_0, ahead_1, bbuf, acc, mask, mask_sem, a_sems, b_sems, ahead_sems):
    mask_copy = pltpu.make_async_copy(mask_hbm, mask, mask_sem)
    mask_copy.start()
    pos = position()
    a_copies, b_copies = [], []
    for k, (start, size) in enumerate(STEPS):
        depth = pl.ds(start, size)
        a_copies.append(pltpu.make_async_copy(adjacency.at[:, depth], masked.at[:, depth], a_sems.at[k]))
        a_copies[k].start()
        b_copies.append(columns_in(operand, pos, FAR, (start, size), bbuf, b_sems.at[k]))
        for copy in b_copies[k]:
            copy.start()
    ahead_copies = columns_in(operand, pos, DIRECT, (0, DEPTH), ahead_0, ahead_sems.at[0])
    ahead_copies += columns_in(operand, pos, MERGED, (0, DEPTH), ahead_1, ahead_sems.at[1])
    mask_copy.wait()
    for k, (start, size) in enumerate(STEPS):
        a_copies[k].wait()
        for i in range(ROWS // TILE):
            for j in range(start // TILE, (start + size) // TILE):
                @pl.when(mask[i, j] == 0)
                def _():
                    masked[i * TILE:(i + 1) * TILE, j * TILE:(j + 1) * TILE] = jnp.zeros((TILE, TILE), BF16)
        for copy in b_copies[k]:
            copy.wait()
        if k == 2:
            for copy in ahead_copies:
                copy.start()
        depth = slice(start, start + size)
        for i in range(ROWS // TILE):
            rows = slice(i * TILE, (i + 1) * TILE)
            part = jnp.dot(masked[rows, depth], bbuf[depth, :], preferred_element_type=F32)
            if k == 0:
                acc[rows, :] = part
            elif k < len(STEPS) - 1:
                acc[rows, :] += part
            else:
                out_a[rows, :] = (acc[rows, :SIDE] + part[:, :SIDE]).astype(BF16)
                out_b[rows, :] = (acc[rows, SIDE:] + part[:, SIDE:]).astype(BF16)
    for copy in ahead_copies:
        copy.wait()


WHOLE = pl.BlockSpec(memory_space=pltpu.VMEM)
IN_HBM = pl.BlockSpec(memory_space=pltpu.HBM)
MM_FLOPS = 2 * ROWS * DEPTH * GROUP
COLUMNS = pltpu.VMEM((DEPTH, GROUP), BF16)


def pinned(space, *arrays):
    return [pltpu.with_memory_space_constraint(x, space) for x in arrays]


def far_block(tile_mask, adjacency, operand):
    return pl.pallas_call(
        far_kernel,
        in_specs=[IN_HBM] * 3,
        out_specs=[WHOLE] * 5,
        scratch_shapes=[
            COLUMNS,
            pltpu.VMEM((ROWS, GROUP), F32),
            pltpu.SMEM((ROWS // TILE, DEPTH // TILE), jnp.int32),
            pltpu.SemaphoreType.DMA,
            pltpu.SemaphoreType.DMA((len(STEPS),)),
            pltpu.SemaphoreType.DMA((len(STEPS), 4)),
            pltpu.SemaphoreType.DMA((2, 4)),
        ],
        out_shape=[pltpu.VMEM((ROWS, DEPTH), BF16)] + [pltpu.VMEM((ROWS, SIDE), BF16)] * 2 + [COLUMNS] * 2,
        compiler_params=pltpu.CompilerParams(vmem_limit_bytes=VMEM_LIMIT),
        cost_estimate=pl.CostEstimate(flops=8 * MM_FLOPS, transcendentals=0, bytes_accessed=20 << 20),
        name="far_block",
    )(*pinned(pltpu.HBM, tile_mask, adjacency, operand))


def near_kernel(merge, masked, columns, *rest):
    arrived, outs = rest[:-2], rest[-2:]
    for i in range(ROWS // TILE):
        rows = slice(i * TILE, (i + 1) * TILE)
        both = jnp.dot(masked[rows], columns[...], preferred_element_type=F32)
        for part, out in enumerate(outs):
            block = both[:, part * SIDE:(part + 1) * SIDE]
            if merge:
                block = block + arrived[part][rows].astype(F32)
            out[rows, :] = block.astype(BF16)


def near_blocks(masked, columns, arrived=()):
    return pl.pallas_call(
        lambda *refs: near_kernel(bool(arrived), *refs),
        in_specs=[WHOLE] * (2 + len(arrived)),
        out_specs=[WHOLE] * 2,
        out_shape=[pltpu.VMEM((ROWS, SIDE), BF16)] * 2,
        compiler_params=pltpu.CompilerParams(vmem_limit_bytes=VMEM_LIMIT),
        cost_estimate=pl.CostEstimate(flops=8 * MM_FLOPS, transcendentals=0, bytes_accessed=0),
        name="near_merged" if arrived else "near_direct",
    )(*pinned(pltpu.VMEM, masked, columns, *arrived))


def own_kernel(masked, operand, out, bbuf, sems):
    pos = position()
    copies = []
    for k, step in enumerate(STEPS):
        copies.append(columns_in(operand, pos, OWN, step, bbuf, sems.at[k]))
        for copy in copies[k]:
            copy.start()
    for k, (start, size) in enumerate(STEPS):
        for copy in copies[k]:
            copy.wait()
        depth = slice(start, start + size)
        block = jnp.dot(masked[:, depth], bbuf[depth, :], preferred_element_type=F32)
        if k == 0:
            out[...] = block
        else:
            out[...] += block


def own_block(masked, operand):
    return pl.pallas_call(
        own_kernel,
        in_specs=[WHOLE, IN_HBM],
        out_specs=WHOLE,
        scratch_shapes=[pltpu.VMEM((DEPTH, GROUP), BF16), pltpu.SemaphoreType.DMA((len(STEPS), 4))],
        out_shape=pltpu.VMEM((ROWS, GROUP), F32),
        compiler_params=pltpu.CompilerParams(vmem_limit_bytes=VMEM_LIMIT),
        cost_estimate=pl.CostEstimate(flops=8 * MM_FLOPS, transcendentals=0, bytes_accessed=4 << 20),
        name="own_block",
    )(*pinned(pltpu.VMEM, masked), *pinned(pltpu.HBM, operand))


def second_kernel(side, own, x, y, *outs):
    for j, out in enumerate(outs):
        lanes = slice(j * LANES, (j + 1) * LANES)
        mine = own[:, side * SIDE + j * LANES:side * SIDE + (j + 1) * LANES]
        out[...] = (mine + x[:, lanes].astype(F32) + y[:, lanes].astype(F32)).astype(out.dtype)


def second_blocks(side, dtypes, own, *arrived):
    return pl.pallas_call(
        lambda *refs: second_kernel(side, *refs),
        in_specs=[WHOLE] * 3,
        out_specs=[WHOLE] * 2,
        out_shape=[pltpu.VMEM((ROWS, LANES), dtype) for dtype in dtypes],
        compiler_params=pltpu.CompilerParams(vmem_limit_bytes=VMEM_LIMIT),
        cost_estimate=pl.CostEstimate(flops=2 * ROWS * SIDE, transcendentals=0, bytes_accessed=0),
        name=f"second_blocks_{side}",
    )(*pinned(pltpu.VMEM, own, *arrived))


def lift_kernel(mine, one, two, three, current, reached, gains):
    lane = lax.broadcasted_iota(jnp.int32, (1, LANES), 1)
    row = jnp.zeros((1, LANES), F32)
    for i in range(ROWS // TILE):
        rows = slice(i * TILE, (i + 1) * TILE)
        logits = mine[rows] + one[rows].astype(F32) + two[rows].astype(F32) + three[rows].astype(F32)
        prior = current[rows].astype(F32)
        lifted = (1.0 - prior) * jax.nn.sigmoid(logits)
        reached[rows, :] = (prior + lifted).astype(BF16)
        total = jnp.sum(jnp.sum(lifted, axis=0, keepdims=True), axis=1, keepdims=True)
        row = row + jnp.where(lane == i, total, 0.0)
    gains[...] = jnp.broadcast_to(row / (TILE * COLS), gains.shape)


def lift(mine, one, two, three, current):
    return pl.pallas_call(
        lift_kernel,
        in_specs=[WHOLE] * 5,
        out_specs=[WHOLE] * 2,
        out_shape=[jax.ShapeDtypeStruct((ROWS, LANES), BF16), jax.ShapeDtypeStruct((128, LANES), F32)],
        compiler_params=pltpu.CompilerParams(vmem_limit_bytes=VMEM_LIMIT),
        name="lift",
    )(mine, one, two, three, current)


def local(adjacency, tile_mask, operand, current):
    row = lax.axis_index("row")
    masked, far_a, far_b, columns, more_columns = far_block(tile_mask, adjacency, operand)
    in_b = moved(far_b, 1, 0)
    in_a = moved(far_a, -1, 0)
    next_a, back_b = near_blocks(masked, columns)
    next_a = moved(next_a, 1, 0)
    back_b = moved(back_b, -1, 0)
    back_a, next_b = near_blocks(masked, more_columns, (in_a, in_b))
    next_b = moved(next_b, 1, 0)
    back_a = moved(back_a, -1, 0)
    own = own_block(masked, operand)
    mine, two = second_blocks(0, (F32, BF16), own, next_a, back_a)
    own, two = lax.optimization_barrier((own, two))
    two = moved(two, 0, 2)
    one, three = second_blocks(1, (BF16, BF16), own, back_b, next_b)
    one = moved(one, 0, 1)
    three = moved(three, 0, -1)
    reached, gains = lift(mine, two, one, three, current)
    gains = lax.all_to_all(gains, ALL, 0, 0, tiled=True)[:, :4]
    sender = lax.broadcasted_iota(jnp.int32, (128, 4, 4), 0) // 16
    earlier = lax.broadcasted_iota(jnp.int32, (128, 4, 4), 1) <= lax.broadcasted_iota(jnp.int32, (128, 4, 4), 2)
    counted = (sender < row) | ((sender == row) & earlier)
    progress = jnp.sum(jnp.where(counted, gains[:, :, None], 0.0), axis=(0, 1))
    return (reached, progress)


def solution(mesh):
    torus = Mesh(mesh.devices.reshape(mesh.shape["row"], 4, 4), ALL)
    in_specs = (P("row", COL), P("row", COL), P(COL, None), P("row", COL))
    out_specs = (P("row", COL), P("row"))
    return jax.shard_map(local, mesh=torus, in_specs=in_specs, out_specs=out_specs, check_vma=False)
```

```python
import jax
import jax.numpy as jnp
from jax import lax
from jax.experimental import pallas as pl
from jax.experimental.pallas import tpu as pltpu
from jax.sharding import Mesh
from jax.sharding import PartitionSpec as P

TILE = 256
COL = ("col_0", "col_1")
ALL = ("row", "col_0", "col_1")
ROWS, DEPTH, COLS, LANES = 1024, 4096, 2048, 128
GROUP = 4 * LANES
SIDE = 2 * LANES
STEPS = ((0, 512), (512, 512), (1024, 1024), (2048, 1024), (3072, 1024))
F32, BF16 = jnp.float32, jnp.bfloat16
VMEM_LIMIT = 16 * 1024 * 1024


def position():
    return lax.axis_index("row") & 1, lax.axis_index("col_0"), lax.axis_index("col_1")


def column_block(pos, first, second):
    core, y, z = pos
    dy = first + core * (second - first)
    dz = second + core * (first - second)
    return ((y + dy) & 3) * 4 + ((z + dz) & 3)


def moved(x, first, second):
    pairs = []
    for dev in range(128):
        row, y, z = dev // 16, dev // 4 % 4, dev % 4
        dy, dz = (first, second) if row % 2 == 0 else (second, first)
        pairs.append((dev, row * 16 + (y + dy) % 4 * 4 + (z + dz) % 4))
    return lax.ppermute(x, ALL, pairs)


def columns_in(operand, pos, blocks, depth, bbuf, sems):
    return [
        pltpu.make_async_copy(
            operand.at[pl.ds(*depth), pl.ds(pl.multiple_of(column_block(pos, *block) * LANES, LANES), LANES)],
            bbuf.at[pl.ds(*depth), pl.ds(j * LANES, LANES)],
            sems.at[j],
        )
        for j, block in enumerate(blocks)
    ]


FAR = ((2, 0), (2, 2), (2, 1), (2, 3))
DIRECT = ((1, 0), (1, 2), (3, 1), (3, 3))
MERGED = ((3, 0), (3, 2), (1, 1), (1, 3))
OWN = ((0, 0), (0, 2), (0, 1), (0, 3))


def far_kernel(mask_hbm, adjacency, operand, masked, out_a, out_b, ahead_0, ahead_1, bbuf, acc, mask, mask_sem, a_sems, b_sems, ahead_sems):
    mask_copy = pltpu.make_async_copy(mask_hbm, mask, mask_sem)
    mask_copy.start()
    pos = position()
    a_copies, b_copies = [], []
    for k, (start, size) in enumerate(STEPS):
        depth = pl.ds(start, size)
        a_copies.append(pltpu.make_async_copy(adjacency.at[:, depth], masked.at[:, depth], a_sems.at[k]))
        a_copies[k].start()
        b_copies.append(columns_in(operand, pos, FAR, (start, size), bbuf, b_sems.at[k]))
        for copy in b_copies[k]:
            copy.start()
    ahead_copies = columns_in(operand, pos, DIRECT, (0, DEPTH), ahead_0, ahead_sems.at[0])
    ahead_copies += columns_in(operand, pos, MERGED, (0, DEPTH), ahead_1, ahead_sems.at[1])
    mask_copy.wait()
    for k, (start, size) in enumerate(STEPS):
        a_copies[k].wait()
        for i in range(ROWS // TILE):
            for j in range(start // TILE, (start + size) // TILE):
                @pl.when(mask[i, j] == 0)
                def _():
                    masked[i * TILE:(i + 1) * TILE, j * TILE:(j + 1) * TILE] = jnp.zeros((TILE, TILE), BF16)
        for copy in b_copies[k]:
            copy.wait()
        if k == 2:
            for copy in ahead_copies:
                copy.start()
        depth = slice(start, start + size)
        for i in range(ROWS // TILE):
            rows = slice(i * TILE, (i + 1) * TILE)
            part = jnp.dot(masked[rows, depth], bbuf[depth, :], preferred_element_type=F32)
            if k == 0:
                acc[rows, :] = part
            elif k < len(STEPS) - 1:
                acc[rows, :] += part
            else:
                out_a[rows, :] = (acc[rows, :SIDE] + part[:, :SIDE]).astype(BF16)
                out_b[rows, :] = (acc[rows, SIDE:] + part[:, SIDE:]).astype(BF16)
    for copy in ahead_copies:
        copy.wait()


WHOLE = pl.BlockSpec(memory_space=pltpu.VMEM)
IN_HBM = pl.BlockSpec(memory_space=pltpu.HBM)
MM_FLOPS = 2 * ROWS * DEPTH * GROUP
COLUMNS = pltpu.VMEM((DEPTH, GROUP), BF16)


def pinned(space, *arrays):
    return [pltpu.with_memory_space_constraint(x, space) for x in arrays]


def far_block(tile_mask, adjacency, operand):
    return pl.pallas_call(
        far_kernel,
        in_specs=[IN_HBM] * 3,
        out_specs=[WHOLE] * 5,
        scratch_shapes=[
            COLUMNS,
            pltpu.VMEM((ROWS, GROUP), F32),
            pltpu.SMEM((ROWS // TILE, DEPTH // TILE), jnp.int32),
            pltpu.SemaphoreType.DMA,
            pltpu.SemaphoreType.DMA((len(STEPS),)),
            pltpu.SemaphoreType.DMA((len(STEPS), 4)),
            pltpu.SemaphoreType.DMA((2, 4)),
        ],
        out_shape=[pltpu.VMEM((ROWS, DEPTH), BF16)] + [pltpu.VMEM((ROWS, SIDE), BF16)] * 2 + [COLUMNS] * 2,
        compiler_params=pltpu.CompilerParams(vmem_limit_bytes=VMEM_LIMIT),
        cost_estimate=pl.CostEstimate(flops=8 * MM_FLOPS, transcendentals=0, bytes_accessed=20 << 20),
        name="far_block",
    )(*pinned(pltpu.HBM, tile_mask, adjacency, operand))


def near_kernel(merge, masked, columns, *rest):
    arrived, outs = rest[:-2], rest[-2:]
    for i in range(ROWS // TILE):
        rows = slice(i * TILE, (i + 1) * TILE)
        both = jnp.dot(masked[rows], columns[...], preferred_element_type=F32)
        for part, out in enumerate(outs):
            block = both[:, part * SIDE:(part + 1) * SIDE]
            if merge:
                block = block + arrived[part][rows].astype(F32)
            out[rows, :] = block.astype(BF16)


def near_blocks(masked, columns, arrived=()):
    return pl.pallas_call(
        lambda *refs: near_kernel(bool(arrived), *refs),
        in_specs=[WHOLE] * (2 + len(arrived)),
        out_specs=[WHOLE] * 2,
        out_shape=[pltpu.VMEM((ROWS, SIDE), BF16)] * 2,
        compiler_params=pltpu.CompilerParams(vmem_limit_bytes=VMEM_LIMIT),
        cost_estimate=pl.CostEstimate(flops=8 * MM_FLOPS, transcendentals=0, bytes_accessed=0),
        name="near_merged" if arrived else "near_direct",
    )(*pinned(pltpu.VMEM, masked, columns, *arrived))


def own_kernel(masked, operand, out, bbuf, sems):
    pos = position()
    copies = []
    for k, step in enumerate(STEPS):
        copies.append(columns_in(operand, pos, OWN, step, bbuf, sems.at[k]))
        for copy in copies[k]:
            copy.start()
    for k, (start, size) in enumerate(STEPS):
        for copy in copies[k]:
            copy.wait()
        depth = slice(start, start + size)
        block = jnp.dot(masked[:, depth], bbuf[depth, :], preferred_element_type=F32)
        if k == 0:
            out[...] = block
        else:
            out[...] += block


def own_block(masked, operand):
    return pl.pallas_call(
        own_kernel,
        in_specs=[WHOLE, IN_HBM],
        out_specs=WHOLE,
        scratch_shapes=[pltpu.VMEM((DEPTH, GROUP), BF16), pltpu.SemaphoreType.DMA((len(STEPS), 4))],
        out_shape=pltpu.VMEM((ROWS, GROUP), F32),
        compiler_params=pltpu.CompilerParams(vmem_limit_bytes=VMEM_LIMIT),
        cost_estimate=pl.CostEstimate(flops=8 * MM_FLOPS, transcendentals=0, bytes_accessed=4 << 20),
        name="own_block",
    )(*pinned(pltpu.VMEM, masked), *pinned(pltpu.HBM, operand))


def second_kernel(side, own, x, y, *rest):
    outs = rest[:2] if side == 0 else rest[-2:]
    if side == 0:
        rest[2][...] = own[:8, :LANES]
    for j, out in enumerate(outs):
        lanes = slice(j * LANES, (j + 1) * LANES)
        mine = own[:, side * SIDE + j * LANES:side * SIDE + (j + 1) * LANES]
        out[...] = (mine + x[:, lanes].astype(F32) + y[:, lanes].astype(F32)).astype(out.dtype)


def second_blocks(side, dtypes, own, *arrived):
    shapes = [(ROWS, LANES), (ROWS, LANES), (8, LANES)]
    return pl.pallas_call(
        lambda *refs: second_kernel(side, *refs),
        in_specs=[WHOLE] * (1 + len(arrived)),
        out_specs=[WHOLE] * len(dtypes),
        out_shape=[pltpu.VMEM(shape, dtype) for shape, dtype in zip(shapes, dtypes)],
        compiler_params=pltpu.CompilerParams(vmem_limit_bytes=VMEM_LIMIT),
        cost_estimate=pl.CostEstimate(flops=2 * ROWS * SIDE, transcendentals=0, bytes_accessed=0),
        name=f"second_blocks_{side}",
    )(*pinned(pltpu.VMEM, own, *arrived))


def lift_kernel(mine, one, two, three, current, reached, gains):
    lane = lax.broadcasted_iota(jnp.int32, (1, LANES), 1)
    running = jnp.zeros((1, LANES), F32)
    whole = jnp.zeros((1, LANES), F32)
    for i in range(ROWS // TILE):
        rows = slice(i * TILE, (i + 1) * TILE)
        logits = mine[rows] + one[rows].astype(F32) + two[rows].astype(F32) + three[rows].astype(F32)
        prior = current[rows].astype(F32)
        lifted = (1.0 - prior) * jax.nn.sigmoid(logits)
        reached[rows, :] = (prior + lifted).astype(BF16)
        total = jnp.sum(jnp.sum(lifted, axis=0, keepdims=True), axis=1, keepdims=True)
        running = running + jnp.where(lane >= i, total, 0.0)
        whole = whole + total
    mine_row = lax.axis_index("row")
    goes_to = lax.broadcasted_iota(jnp.int32, gains.shape, 0) // 16
    sums = jnp.where(goes_to == mine_row, running, jnp.where(goes_to > mine_row, whole, 0.0))
    gains[...] = sums / (TILE * COLS)


def lift(mine, one, two, three, current):
    return pl.pallas_call(
        lift_kernel,
        in_specs=[WHOLE] * 5,
        out_specs=[WHOLE] * 2,
        out_shape=[jax.ShapeDtypeStruct((ROWS, LANES), BF16), jax.ShapeDtypeStruct((128, LANES), F32)],
        compiler_params=pltpu.CompilerParams(vmem_limit_bytes=VMEM_LIMIT),
        name="lift",
    )(mine, one, two, three, current)


def local(adjacency, tile_mask, operand, current):
    masked, far_a, far_b, columns, more_columns = far_block(tile_mask, adjacency, operand)
    in_b = moved(far_b, 1, 0)
    in_a = moved(far_a, -1, 0)
    next_a, back_b = near_blocks(masked, columns)
    next_a = moved(next_a, 1, 0)
    back_b = moved(back_b, -1, 0)
    back_a, next_b = near_blocks(masked, more_columns, (in_a, in_b))
    next_b = moved(next_b, 1, 0)
    back_a = moved(back_a, -1, 0)
    own = own_block(masked, operand)
    mine, two, token = second_blocks(0, (F32, BF16, F32), own, next_a, back_a)
    token = lax.ppermute(token, ALL, [(dev, dev ^ 16) for dev in range(128)])
    two = moved(two, 0, 2)
    one, three = second_blocks(1, (BF16, BF16), own, back_b, next_b, token)
    one = moved(one, 0, 1)
    three = moved(three, 0, -1)
    reached, gains = lift(mine, two, one, three, current)
    progress = jnp.sum(lax.all_to_all(gains, ALL, 0, 0, tiled=True)[:, :ROWS // TILE], axis=0)
    return (reached, progress)


def solution(mesh):
    torus = Mesh(mesh.devices.reshape(mesh.shape["row"], 4, 4), ALL)
    in_specs = (P("row", COL), P("row", COL), P(COL, None), P("row", COL))
    out_specs = (P("row", COL), P("row"))
    return jax.shard_map(local, mesh=torus, in_specs=in_specs, out_specs=out_specs, check_vma=False)
```

```python
import jax
import jax.numpy as jnp
from jax import lax
from jax.experimental import pallas as pl
from jax.experimental.pallas import tpu as pltpu
from jax.sharding import Mesh
from jax.sharding import PartitionSpec as P

TILE = 256
COL = ("col_0", "col_1")
ALL = ("row", "col_0", "col_1")
ROWS, DEPTH, COLS, LANES = 1024, 4096, 2048, 128
GROUP = 4 * LANES
SIDE = 2 * LANES
STEPS = ((0, 512), (512, 512), (1024, 1024), (2048, 1024), (3072, 1024))
F32, BF16 = jnp.float32, jnp.bfloat16
VMEM_LIMIT = 16 * 1024 * 1024


def position():
    return lax.axis_index("row") & 1, lax.axis_index("col_0"), lax.axis_index("col_1")


def column_block(pos, first, second):
    core, y, z = pos
    dy = first + core * (second - first)
    dz = second + core * (first - second)
    return ((y + dy) & 3) * 4 + ((z + dz) & 3)


def moved(x, first, second):
    pairs = []
    for dev in range(128):
        row, y, z = dev // 16, dev // 4 % 4, dev % 4
        dy, dz = (first, second) if row % 2 == 0 else (second, first)
        pairs.append((dev, row * 16 + (y + dy) % 4 * 4 + (z + dz) % 4))
    return lax.ppermute(x, ALL, pairs)


def columns_in(operand, pos, blocks, depth, bbuf, sems):
    return [
        pltpu.make_async_copy(
            operand.at[pl.ds(*depth), pl.ds(pl.multiple_of(column_block(pos, *block) * LANES, LANES), LANES)],
            bbuf.at[pl.ds(*depth), pl.ds(j * LANES, LANES)],
            sems.at[j],
        )
        for j, block in enumerate(blocks)
    ]


FAR = ((2, 0), (2, 2), (2, 1), (2, 3))
DIRECT = ((1, 0), (1, 2), (3, 1), (3, 3))
MERGED = ((3, 0), (3, 2), (1, 1), (1, 3))
OWN = ((0, 0), (0, 2), (0, 1), (0, 3))


def far_kernel(mask_hbm, adjacency, operand, masked, out_a, out_b, ahead_0, ahead_1, bbuf, acc, mask, mask_sem, a_sems, b_sems, ahead_sems):
    mask_copy = pltpu.make_async_copy(mask_hbm, mask, mask_sem)
    mask_copy.start()
    pos = position()
    a_copies, b_copies = [], []
    for k, (start, size) in enumerate(STEPS):
        depth = pl.ds(start, size)
        a_copies.append(pltpu.make_async_copy(adjacency.at[:, depth], masked.at[:, depth], a_sems.at[k]))
        a_copies[k].start()
        b_copies.append(columns_in(operand, pos, FAR, (start, size), bbuf, b_sems.at[k]))
        for copy in b_copies[k]:
            copy.start()
    ahead_copies = columns_in(operand, pos, DIRECT, (0, DEPTH), ahead_0, ahead_sems.at[0])
    ahead_copies += columns_in(operand, pos, MERGED, (0, DEPTH), ahead_1, ahead_sems.at[1])
    mask_copy.wait()
    for k, (start, size) in enumerate(STEPS):
        a_copies[k].wait()
        for i in range(ROWS // TILE):
            for j in range(start // TILE, (start + size) // TILE):
                @pl.when(mask[i, j] == 0)
                def _():
                    masked[i * TILE:(i + 1) * TILE, j * TILE:(j + 1) * TILE] = jnp.zeros((TILE, TILE), BF16)
        for copy in b_copies[k]:
            copy.wait()
        if k == 2:
            for copy in ahead_copies:
                copy.start()
        depth = slice(start, start + size)
        for i in range(ROWS // TILE):
            rows = slice(i * TILE, (i + 1) * TILE)
            part = jnp.dot(masked[rows, depth], bbuf[depth, :], preferred_element_type=F32)
            if k == 0:
                acc[rows, :] = part
            elif k < len(STEPS) - 1:
                acc[rows, :] += part
            else:
                out_a[rows, :] = (acc[rows, :SIDE] + part[:, :SIDE]).astype(BF16)
                out_b[rows, :] = (acc[rows, SIDE:] + part[:, SIDE:]).astype(BF16)
    for copy in ahead_copies:
        copy.wait()


WHOLE = pl.BlockSpec(memory_space=pltpu.VMEM)
IN_HBM = pl.BlockSpec(memory_space=pltpu.HBM)
MM_FLOPS = 2 * ROWS * DEPTH * GROUP
COLUMNS = pltpu.VMEM((DEPTH, GROUP), BF16)


def pinned(space, *arrays):
    return [pltpu.with_memory_space_constraint(x, space) for x in arrays]


def far_block(tile_mask, adjacency, operand):
    return pl.pallas_call(
        far_kernel,
        in_specs=[IN_HBM] * 3,
        out_specs=[WHOLE] * 5,
        scratch_shapes=[
            COLUMNS,
            pltpu.VMEM((ROWS, GROUP), F32),
            pltpu.SMEM((ROWS // TILE, DEPTH // TILE), jnp.int32),
            pltpu.SemaphoreType.DMA,
            pltpu.SemaphoreType.DMA((len(STEPS),)),
            pltpu.SemaphoreType.DMA((len(STEPS), 4)),
            pltpu.SemaphoreType.DMA((2, 4)),
        ],
        out_shape=[pltpu.VMEM((ROWS, DEPTH), BF16)] + [pltpu.VMEM((ROWS, SIDE), BF16)] * 2 + [COLUMNS] * 2,
        compiler_params=pltpu.CompilerParams(vmem_limit_bytes=VMEM_LIMIT),
        cost_estimate=pl.CostEstimate(flops=8 * MM_FLOPS, transcendentals=0, bytes_accessed=20 << 20),
        name="far_block",
    )(*pinned(pltpu.HBM, tile_mask, adjacency, operand))


def near_kernel(merge, masked, columns, *rest):
    arrived, outs = rest[:-2], rest[-2:]
    for i in range(ROWS // TILE):
        rows = slice(i * TILE, (i + 1) * TILE)
        both = jnp.dot(masked[rows], columns[...], preferred_element_type=F32)
        for part, out in enumerate(outs):
            block = both[:, part * SIDE:(part + 1) * SIDE]
            if merge:
                block = block + arrived[part][rows].astype(F32)
            out[rows, :] = block.astype(BF16)


def near_blocks(masked, columns, arrived=()):
    return pl.pallas_call(
        lambda *refs: near_kernel(bool(arrived), *refs),
        in_specs=[WHOLE] * (2 + len(arrived)),
        out_specs=[WHOLE] * 2,
        out_shape=[pltpu.VMEM((ROWS, SIDE), BF16)] * 2,
        compiler_params=pltpu.CompilerParams(vmem_limit_bytes=VMEM_LIMIT),
        cost_estimate=pl.CostEstimate(flops=8 * MM_FLOPS, transcendentals=0, bytes_accessed=0),
        name="near_merged" if arrived else "near_direct",
    )(*pinned(pltpu.VMEM, masked, columns, *arrived))


def own_kernel(masked, operand, out, bbuf, sems):
    pos = position()
    copies = []
    for k, step in enumerate(STEPS):
        copies.append(columns_in(operand, pos, OWN, step, bbuf, sems.at[k]))
        for copy in copies[k]:
            copy.start()
    for k, (start, size) in enumerate(STEPS):
        for copy in copies[k]:
            copy.wait()
        depth = slice(start, start + size)
        block = jnp.dot(masked[:, depth], bbuf[depth, :], preferred_element_type=F32)
        if k == 0:
            out[...] = block
        else:
            out[...] += block


def own_block(masked, operand):
    return pl.pallas_call(
        own_kernel,
        in_specs=[WHOLE, IN_HBM],
        out_specs=WHOLE,
        scratch_shapes=[pltpu.VMEM((DEPTH, GROUP), BF16), pltpu.SemaphoreType.DMA((len(STEPS), 4))],
        out_shape=pltpu.VMEM((ROWS, GROUP), F32),
        compiler_params=pltpu.CompilerParams(vmem_limit_bytes=VMEM_LIMIT),
        cost_estimate=pl.CostEstimate(flops=8 * MM_FLOPS, transcendentals=0, bytes_accessed=4 << 20),
        name="own_block",
    )(*pinned(pltpu.VMEM, masked), *pinned(pltpu.HBM, operand))


def second_kernel(side, own, x, y, *rest):
    outs = rest[:2] if side == 0 else rest[-2:]
    if side == 0:
        rest[2][...] = own[:8, :LANES]
    for j, out in enumerate(outs):
        lanes = slice(j * LANES, (j + 1) * LANES)
        mine = own[:, side * SIDE + j * LANES:side * SIDE + (j + 1) * LANES]
        out[...] = (mine + x[:, lanes].astype(F32) + y[:, lanes].astype(F32)).astype(out.dtype)


def second_blocks(side, dtypes, own, *arrived):
    shapes = [(ROWS, LANES), (ROWS, LANES), (8, LANES)]
    return pl.pallas_call(
        lambda *refs: second_kernel(side, *refs),
        in_specs=[WHOLE] * (1 + len(arrived)),
        out_specs=[WHOLE] * len(dtypes),
        out_shape=[pltpu.VMEM(shape, dtype) for shape, dtype in zip(shapes, dtypes)],
        compiler_params=pltpu.CompilerParams(vmem_limit_bytes=VMEM_LIMIT),
        cost_estimate=pl.CostEstimate(flops=2 * ROWS * SIDE, transcendentals=0, bytes_accessed=0),
        name=f"second_blocks_{side}",
    )(*pinned(pltpu.VMEM, own, *arrived))


def lift_kernel(mine, one, two, three, current, reached, gains):
    lane = lax.broadcasted_iota(jnp.int32, (1, LANES), 1)
    running = jnp.zeros((1, LANES), F32)
    whole = jnp.zeros((1, LANES), F32)
    for i in range(ROWS // TILE):
        rows = slice(i * TILE, (i + 1) * TILE)
        logits = mine[rows] + one[rows].astype(F32) + two[rows].astype(F32) + three[rows].astype(F32)
        prior = current[rows].astype(F32)
        lifted = (1.0 - prior) * jax.nn.sigmoid(logits)
        reached[rows, :] = (prior + lifted).astype(BF16)
        total = jnp.sum(jnp.sum(lifted, axis=0, keepdims=True), axis=1, keepdims=True)
        running = running + jnp.where(lane >= i, total, 0.0)
        whole = whole + total
    mine_row = lax.axis_index("row")
    goes_to = lax.broadcasted_iota(jnp.int32, gains.shape, 0) // 16
    sums = jnp.where(goes_to == mine_row, running, jnp.where(goes_to > mine_row, whole, 0.0))
    gains[...] = sums / (TILE * COLS)


def lift(mine, one, two, three, current):
    return pl.pallas_call(
        lift_kernel,
        in_specs=[WHOLE] * 5,
        out_specs=[WHOLE] * 2,
        out_shape=[jax.ShapeDtypeStruct((ROWS, LANES), BF16), jax.ShapeDtypeStruct((128, LANES), F32)],
        compiler_params=pltpu.CompilerParams(vmem_limit_bytes=VMEM_LIMIT),
        name="lift",
    )(mine, one, two, three, current)


def local(adjacency, tile_mask, operand, current):
    masked, far_a, far_b, columns, more_columns = far_block(tile_mask, adjacency, operand)
    in_b = moved(far_b, 1, 0)
    in_a = moved(far_a, -1, 0)
    next_a, back_b = near_blocks(masked, columns)
    next_a = moved(next_a, 1, 0)
    back_b = moved(back_b, -1, 0)
    back_a, next_b = near_blocks(masked, more_columns, (in_a, in_b))
    next_b = moved(next_b, 1, 0)
    back_a = moved(back_a, -1, 0)
    own = own_block(masked, operand)
    mine, two, token = second_blocks(0, (F32, BF16, F32), own, next_a, back_a)
    token = lax.ppermute(token, ALL, [(dev, dev ^ 16) for dev in range(128)])
    two, token = lax.optimization_barrier((two, token))
    two = moved(two, 0, 2)
    one, three = second_blocks(1, (BF16, BF16), own, back_b, next_b, token)
    one = moved(one, 0, 1)
    three = moved(three, 0, -1)
    reached, gains = lift(mine, two, one, three, current)
    progress = jnp.sum(lax.all_to_all(gains, ALL, 0, 0, tiled=True)[:, :ROWS // TILE], axis=0)
    return (reached, progress)


def solution(mesh):
    torus = Mesh(mesh.devices.reshape(mesh.shape["row"], 4, 4), ALL)
    in_specs = (P("row", COL), P("row", COL), P(COL, None), P("row", COL))
    out_specs = (P("row", COL), P("row"))
    return jax.shard_map(local, mesh=torus, in_specs=in_specs, out_specs=out_specs, check_vma=False)
```
